32 devices in a mesh: group: 2 (over x), ctx: 16 (over z, y, core).
Axes of the slice: x: 2, y: 2, z: 4, core: 2. Of those that a mesh axis runs over, the one named last changes fastest.
Arguments:
- queries: bfloat16 [256, 8, 8192], P(('group', 'ctx')), parts along dimension 0, may hold values from -40 to 40
- kv_cache: bfloat16 [32, 2, 512, 1024], P(('group', 'ctx')), parts along dimension 0, may hold values from -16 to 16
- page_counts: int32 [16], P('group'), parts along dimension 0, may hold values from 1 to 6, as said below
- doc_ids: int32 [16], P('group'), parts along dimension 0, may hold values from 0 to 7, each once
Outputs:
- attended: bfloat16 [256, 8, 8192], P(('group', 'ctx')), parts along dimension 0
The draws below stay inside these ranges and needn't reach their ends.
There are 2 independent parts, one for each index of `group`. The reference program is written for one: setup_inputs(seed, part) draws one part's arguments, and reference() takes and returns one part's arrays. A program takes and returns all parts, laid end to end along the dimension named above; each array names one. Nothing has to cross between parts.
Inputs may be any that keep to these rules, and one draw needn't show every extreme that they name: `page_counts`: the counts sum to 16; every document holds at least 1 pages, some document exactly 1, and some document exactly 6. `doc_ids`: every document is named by exactly one question block.
All inputs are finite; a program needn't handle non-finite values.
Results may differ from the reference program's by a relative error of at most 0.0031.
Values may be sent and summed in bfloat16 or wider, within the bound.
A program may use at most 128 MiB of HBM per device.

```python
import jax
import jax.numpy as jnp
from jax import lax

HEADS = 64
KV_HEADS = 8
HEAD_DIM = 128
DOCS = 8
QUERY_TOK = 128
PAGE_TOK = 512
PAGES_DEV = 1
PAGES = 16


def draw_queries(key, part):
    width = HEADS * HEAD_DIM
    base = jax.random.truncated_normal(jax.random.fold_in(key, 21), -4.0, 4.0, (QUERY_TOK, DOCS, width), jnp.float32) * 2.0
    return base.astype(jnp.bfloat16)


def draw_kv_cache(key, part):
    noise = jax.random.truncated_normal(jax.random.fold_in(key, 31), -4.0, 4.0, (PAGES, 2, PAGE_TOK, KV_HEADS * HEAD_DIM), jnp.float32)
    key_part = noise[:, 0]
    value_part = 4.0 * noise[:, 1]
    return jnp.stack([key_part, value_part], axis=1).astype(jnp.bfloat16)


def draw_page_counts(key, part):
    most_pages = 3 * PAGES // DOCS
    middle = DOCS - 2
    rest_pages = PAGES - most_pages - PAGES_DEV
    extra_pages = rest_pages - middle * PAGES_DEV
    share_base = extra_pages // middle
    leftover = extra_pages % middle
    shares = share_base + (jnp.arange(middle, dtype=jnp.int32) < leftover).astype(jnp.int32)
    pair_count = middle // 2
    spread = max(0, min(share_base, most_pages - PAGES_DEV - share_base - 1))
    delta = jax.random.randint(jax.random.fold_in(key, 43), (pair_count,), 0, spread + 1).astype(jnp.int32)
    moved = jnp.zeros((middle,), jnp.int32)
    moved = moved.at[0:2 * pair_count:2].add(delta)
    moved = moved.at[1:2 * pair_count:2].add(-delta)
    middle_counts = PAGES_DEV + shares + moved
    counts = jnp.concatenate([jnp.full((1,), most_pages, jnp.int32), jnp.full((1,), PAGES_DEV, jnp.int32), middle_counts])
    shuffle = jax.random.permutation(jax.random.fold_in(key, 42), DOCS)
    return counts[shuffle].astype(jnp.int32)


def setup_inputs(seed: int = 0, part: int = 0) -> dict:
    key_list = jax.random.split(jax.random.key(seed), 5)
    own_keys = jax.random.split(jax.random.fold_in(key_list[4], part), 5)
    return {
        "queries": draw_queries(jax.random.fold_in(jax.random.fold_in(key_list[4], part), 71), part),
        "kv_cache": draw_kv_cache(jax.random.fold_in(jax.random.fold_in(key_list[4], part), 71), part),
        "page_counts": draw_page_counts(jax.random.fold_in(jax.random.fold_in(key_list[4], part), 71), part),
        "doc_ids": jax.random.permutation(own_keys[3], DOCS).astype(jnp.int32),
    }


def page_partial(rows, page_kv):
    tokens = rows.shape[0]
    kv_heads = page_kv.shape[-1] // HEAD_DIM
    groups = rows.shape[-1] // (kv_heads * HEAD_DIM)
    grouped = rows.astype(jnp.float32).reshape(tokens, kv_heads, groups, HEAD_DIM)
    keys = page_kv[0].astype(jnp.float32).reshape(-1, kv_heads, HEAD_DIM)
    values = page_kv[1].astype(jnp.float32).reshape(-1, kv_heads, HEAD_DIM)
    scores = jnp.einsum("qhgd,khd->qhgk", grouped, keys, precision=lax.Precision.HIGHEST) * (HEAD_DIM ** -0.5)
    row_max = jnp.max(scores, axis=-1)
    expo = jnp.exp(scores - row_max[..., None])
    row_sum = jnp.sum(expo, axis=-1)
    weights = lax.optimization_barrier(expo.astype(jnp.bfloat16)).astype(jnp.float32)
    mixed = jnp.einsum("qhgk,khd->qhgd", weights, values, precision=lax.Precision.HIGHEST)
    return row_max.reshape(tokens, -1), row_sum.reshape(tokens, -1), mixed.reshape(tokens, -1)


def reference(queries, kv_cache, page_counts, doc_ids):
    doc_ends = jnp.cumsum(page_counts).astype(jnp.int32)
    block_order = jnp.arange(DOCS, dtype=jnp.int32)
    width = HEADS * HEAD_DIM

    def visit(carry, page):
        big_max, big_sum, big_out = carry
        page_doc = jnp.sum((page >= doc_ends).astype(jnp.int32))
        block = jnp.sum(jnp.where(doc_ids == page_doc, block_order, 0)).astype(jnp.int32)
        rows = lax.dynamic_index_in_dim(queries, block, 1, keepdims=False)
        page_kv = lax.dynamic_index_in_dim(kv_cache, page.astype(jnp.int32), 0, keepdims=False)
        row_max, row_sum, mixed = page_partial(rows, page_kv)
        old_max = lax.dynamic_index_in_dim(big_max, block, 0, keepdims=False)
        old_sum = lax.dynamic_index_in_dim(big_sum, block, 0, keepdims=False)
        old_out = lax.dynamic_index_in_dim(big_out, block, 0, keepdims=False)
        new_max = jnp.maximum(old_max, row_max)
        keep_old = jnp.exp(old_max - new_max)
        keep_new = jnp.exp(row_max - new_max)
        new_sum = keep_old * old_sum + keep_new * row_sum
        tokens = rows.shape[0]
        new_out = (keep_old[..., None] * old_out.reshape(tokens, HEADS, HEAD_DIM)
                   + keep_new[..., None] * mixed.reshape(tokens, HEADS, HEAD_DIM)).reshape(tokens, width)
        big_max = lax.dynamic_update_index_in_dim(big_max, new_max, block, 0)
        big_sum = lax.dynamic_update_index_in_dim(big_sum, new_sum, block, 0)
        big_out = lax.dynamic_update_index_in_dim(big_out, new_out, block, 0)
        return (big_max, big_sum, big_out), None

    start = (jnp.full((DOCS, QUERY_TOK, HEADS), -1e30, jnp.float32),
             jnp.zeros((DOCS, QUERY_TOK, HEADS), jnp.float32),
             jnp.zeros((DOCS, QUERY_TOK, width), jnp.float32))
    pages = jnp.arange(PAGES, dtype=jnp.int32)
    (big_max, big_sum, big_out), unused = lax.scan(visit, start, pages)
    normed = big_out.reshape(DOCS, QUERY_TOK, HEADS, HEAD_DIM) / big_sum[..., None]
    normed = jnp.transpose(normed.reshape(DOCS, QUERY_TOK, width), (1, 0, 2))
    return normed.astype(jnp.bfloat16)
```

```python
import functools

import jax
import jax.numpy as jnp
from jax import lax
from jax.experimental import pallas as pl
from jax.experimental.pallas import tpu as pltpu
from jax.sharding import PartitionSpec as P

HEAD_DIM = 128
CHUNKS = 4


def attend_kernel(
    peers, counts, doc_ids, q_hbm, kv_hbm, out_hbm,
    raw_buf, doc_buf, send_buf, q_buf, o_buf, got_buf, s_buf, stats_buf, w_buf, top_buf,
    run_buf, out_buf, kv_buf, ends, page_doc, page_block, fresh,
    raw_sem, q_send, q_recv, o_send, o_recv, s_send, s_recv, own_q_sem, own_o_sem, own_s_sem,
    kv_sem, out_sem,
):
    chunks, _, rows, wide = q_buf.shape
    blocks = counts.shape[0]
    me = lax.axis_index("ctx")
    tokens = peers * rows
    heads_chunk = wide // HEAD_DIM
    kv_heads = kv_buf.shape[2] // HEAD_DIM
    groups = chunks * heads_chunk // kv_heads
    mesh_id = pl.DeviceIdType.MESH

    barrier = pltpu.get_barrier_semaphore()

    @pl.loop(1, peers)
    def _(k):
        pl.semaphore_signal(
            barrier, inc=1, device_id={"ctx": lax.rem(me + k, peers)}, device_id_type=mesh_id
        )

    def columns(c):
        return pl.ds(c * wide, wide)

    raw_copies = [
        pltpu.make_async_copy(q_hbm.at[:, :, columns(c)], raw_buf.at[c], raw_sem.at[c])
        for c in range(chunks)
    ]
    for copy in raw_copies:
        copy.start()
    kv_copy = pltpu.make_async_copy(kv_hbm.at[0], kv_buf, kv_sem)
    kv_copy.start()

    end = 0
    for j in range(blocks):
        end = end + counts[j]
        ends[j] = end

    def locate(n, before):
        doc = 0
        for j in range(blocks):
            doc = doc + (n >= ends[j]).astype(jnp.int32)
        block = 0
        for j in range(1, blocks):
            block = block + jnp.where(doc_ids[j] == doc, j, 0)
        page_doc[n] = doc
        page_block[n] = block
        fresh[n] = (doc != before).astype(jnp.int32)
        return doc

    lax.fori_loop(0, peers, locate, jnp.int32(-1))
    fresh[peers] = 1

    def send(src, dst, send_sem, recv_sem):
        @pl.loop(1, peers)
        def _(k):
            peer = lax.rem(me + k, peers)
            pltpu.make_async_remote_copy(
                src_ref=src.at[peer], dst_ref=dst.at[me], send_sem=send_sem,
                recv_sem=recv_sem, device_id={"ctx": peer}, device_id_type=mesh_id,
            ).start()

    def drain(ref, sem):
        part = ref.at[pl.ds(0, peers - 1)]
        pltpu.make_async_copy(part, part, sem).wait()

    own_q, own_o = [], []
    for c in range(chunks):
        raw_copies[c].wait()
        raw = raw_buf[c].astype(jnp.float32)
        doc_buf[c] = jnp.swapaxes(raw, 0, 1).astype(jnp.bfloat16)

        @pl.loop(0, peers)
        def _(n):
            send_buf[c, n] = doc_buf[c, page_block[n]]

        if c == 0:
            pl.semaphore_wait(barrier, peers - 1)
        send(send_buf.at[c], q_buf.at[c], q_send.at[c], q_recv.at[c])
        copy = pltpu.make_async_copy(send_buf.at[c, me], q_buf.at[c, me], own_q_sem.at[c])
        copy.start()
        own_q.append(copy)

    s_buf[...] = jnp.zeros_like(s_buf)
    kv_copy.wait()
    lane = lax.broadcasted_iota(jnp.int32, (tokens, 128), 1)
    own_s = pltpu.make_async_copy(s_buf.at[me], stats_buf.at[me], own_s_sem)
    for c in range(chunks):
        own_q[c].wait()
        drain(q_buf.at[c], q_recv.at[c])

        def head(j, carry):
            lanes = pl.ds(pl.multiple_of(j * HEAD_DIM, HEAD_DIM), HEAD_DIM)
            h = c * heads_chunk + j
            kv_lanes = pl.ds(pl.multiple_of(h // groups * HEAD_DIM, HEAD_DIM), HEAD_DIM)
            q = q_buf[c, :, :, lanes].astype(jnp.float32).reshape(tokens, HEAD_DIM)
            s = lax.dot_general(
                q.astype(jnp.bfloat16), kv_buf[0, :, kv_lanes], (((1,), (1,)), ((), ())),
                preferred_element_type=jnp.float32,
            ) * HEAD_DIM ** (-0.5)
            top = jnp.max(s, axis=-1, keepdims=True)
            p = jnp.exp(s - top)
            total = jnp.sum(p, axis=-1, keepdims=True)
            o = jnp.dot(
                p.astype(jnp.bfloat16), kv_buf[1, :, kv_lanes],
                preferred_element_type=jnp.float32,
            ) / total
            o_buf[c, :, :, lanes] = o.reshape(peers, rows, HEAD_DIM).astype(jnp.bfloat16)
            old = s_buf[...].reshape(tokens, 128)
            new = jnp.where(lane == h, top, jnp.where(lane == h + 64, total, old))
            s_buf[...] = new.reshape(peers, rows, 128)
            return carry

        lax.fori_loop(0, heads_chunk, head, 0)
        if c == chunks - 1:
            send(s_buf, stats_buf, s_send, s_recv)
            own_s.start()
        send(o_buf.at[c], got_buf.at[c], o_send.at[c], o_recv.at[c])
        copy = pltpu.make_async_copy(o_buf.at[c, me], got_buf.at[c, me], own_o_sem.at[c])
        copy.start()
        own_o.append(copy)

    own_s.wait()
    drain(stats_buf, s_recv)

    def forward(n, top):
        mine = stats_buf[n]
        top = jnp.where(fresh[n] == 1, mine, jnp.maximum(top, mine))
        top_buf[n] = top
        return top

    def backward(i, top):
        n = peers - 1 - i
        top = jnp.where(fresh[n + 1] == 1, top_buf[n], top)
        top_buf[n] = top
        return top

    def weigh(n, total):
        mine = stats_buf[n]
        w = jnp.exp(mine - top_buf[n]) * pltpu.roll(mine, 128 - 64, 1)
        w_buf[n] = w
        total = jnp.where(fresh[n] == 1, w, total + w)
        top_buf[n] = total
        return total

    def norm(i, total):
        n = peers - 1 - i
        total = jnp.where(fresh[n + 1] == 1, top_buf[n], total)
        w_buf[n] = w_buf[n] / total
        return total

    zero = jnp.zeros((rows, 128), jnp.float32)
    lax.fori_loop(0, peers, forward, zero)
    lax.fori_loop(0, peers, backward, zero)
    lax.fori_loop(0, peers, weigh, zero)
    lax.fori_loop(0, peers, norm, zero)

    outs = []
    for c in range(chunks):
        own_o[c].wait()
        drain(got_buf.at[c], o_recv.at[c])

        def visit(n, acc):
            w = w_buf[n]
            w = jnp.concatenate(
                [
                    jnp.broadcast_to(w[:, h:h + 1], (rows, HEAD_DIM))
                    for h in range(c * heads_chunk, (c + 1) * heads_chunk)
                ],
                axis=1,
            )
            mine = w * got_buf[c, n].astype(jnp.float32)
            acc = jnp.where(fresh[n] == 1, mine, acc + mine)
            run_buf[n] = acc
            return acc

        lax.fori_loop(0, peers, visit, jnp.zeros((rows, wide), jnp.float32), unroll=2)
        picked = jnp.stack([run_buf[jnp.clip(ends[doc_ids[b]] - 1, 0, peers - 1)] for b in range(blocks)], axis=0)
        out_buf[c] = jnp.swapaxes(picked, 0, 1).astype(jnp.bfloat16)
        copy = pltpu.make_async_copy(out_buf.at[c], out_hbm.at[:, :, columns(c)], out_sem.at[c])
        copy.start()
        outs.append(copy)
    drain(s_buf, s_send)
    for c in range(chunks):
        drain(send_buf.at[c], q_send.at[c])
        drain(o_buf.at[c], o_send.at[c])
        outs[c].wait()


STEPS = 16
LAG = 4
GROUPS = 4
FAR = -1e30


def merge(o1, l1, o2, l2):
    top = jnp.maximum(l1, l2)
    w1, w2 = jnp.exp(l1 - top), jnp.exp(l2 - top)
    out = (w1 * o1.astype(jnp.float32) + w2 * o2.astype(jnp.float32)) / (w1 + w2)
    return out.astype(jnp.bfloat16)


def join(l1, l2):
    top = jnp.maximum(l1, l2)
    return top + jnp.log(jnp.exp(l1 - top) + jnp.exp(l2 - top))


def to_row(col, first):
    shape = (col.shape[0], 128)
    hit = lax.broadcasted_iota(jnp.int32, shape, 1) == lax.broadcasted_iota(jnp.int32, shape, 0) + first
    return jnp.sum(jnp.where(hit, col, 0.0), axis=0, keepdims=True)


def to_col(row, first, count):
    shape = (count, 128)
    hit = lax.broadcasted_iota(jnp.int32, shape, 1) == lax.broadcasted_iota(jnp.int32, shape, 0) + first
    return jnp.sum(jnp.where(hit, row, 0.0), axis=1, keepdims=True)


def pick(parts, index):
    got = parts[0]
    for n in range(1, len(parts)):
        got = jnp.where(index == n, parts[n], got)
    return got


def line_kernel(
    counts, doc_ids, q_hbm, kv_hbm, out_hbm,
    raw, kv, blk, s1r, xs, xr, xls, xlr, cs, cr, dr, dlr, fs, fr, fls, flr,
    qt, run, lse, oh, lh, fin, ends,
    q_ssem, q_rsem, q_own, kv_ssem, kv_rsem, kv_own, s_ssem, s_rsem, x_ssem, x_rsem, xl_ssem, xl_rsem,
    c_ssem, c_rsem, d_ssem, d_rsem, dl_ssem, dl_rsem, f_ssem, f_rsem, fl_ssem, fl_rsem,
    o_ssem, o_rsem, o_own,
):
    blocks = counts.shape[0]
    rounds = STEPS + LAG
    me = lax.axis_index("ctx")
    z, mine = me // 4, me % 4
    upper = z // 2
    hub = (z == 1) | (z == 2)
    leaf = (z == 0) | (z == 3)
    away = jnp.where((z == 0) | (z == 2), me + 4, me - 4)
    across = jnp.where(z == 1, me + 4, me - 4)
    mesh_id = pl.DeviceIdType.MESH

    def plane(k):
        return z * 4 + (mine + k) % 4, (mine + k) % 4

    barrier = pltpu.get_barrier_semaphore()
    for k in range(1, 4):
        pl.semaphore_signal(barrier, inc=1, device_id={"ctx": plane(k)[0]}, device_id_type=mesh_id)
    pl.semaphore_signal(barrier, inc=1, device_id={"ctx": away}, device_id_type=mesh_id)

    @pl.when(hub)
    def _():
        pl.semaphore_signal(barrier, inc=1, device_id={"ctx": across}, device_id_type=mesh_id)

    def lanes(i, g):
        return pl.ds(pl.multiple_of(i * 2048 + g * 512, 128), 512)

    def heads(i, h):
        return pl.ds(pl.multiple_of(i * 256 + h * 128, 128), 128)

    own = []
    for g in range(GROUPS):
        own.append(pltpu.make_async_copy(q_hbm.at[:, :, lanes(mine, g)], raw.at[g, mine], q_own.at[g]))
    for h in range(2):
        own.append(pltpu.make_async_copy(kv_hbm.at[0, :, :, heads(mine, h)], kv.at[h, mine], kv_own.at[h]))
    for copy in own:
        copy.start()

    def remote(src, dst, ssem, rsem, peer):
        pltpu.make_async_remote_copy(
            src_ref=src, dst_ref=dst, send_sem=ssem, recv_sem=rsem,
            device_id={"ctx": peer}, device_id_type=mesh_id,
        ).start()

    def wait(ref, sem):
        pltpu.make_async_copy(ref, ref, sem).wait()

    @pl.when(hub)
    def _():
        pl.semaphore_wait(barrier, 5)

    @pl.when(leaf)
    def _():
        pl.semaphore_wait(barrier, 4)

    def send_group(g):
        for k in range(1, 4):
            peer, i = plane(k)
            remote(q_hbm.at[:, :, lanes(i, g)], raw.at[g, mine], q_ssem, q_rsem.at[g], peer)

    def send_kv(h):
        for k in range(1, 4):
            peer, i = plane(k)
            remote(kv_hbm.at[0, :, :, heads(i, h)], kv.at[h, mine], kv_ssem, kv_rsem.at[h], peer)

    send_group(0)
    send_kv(0)
    send_group(1)
    send_group(2)
    send_group(3)
    send_kv(1)

    end = 0
    for j in range(blocks):
        end = end + counts[j]
        ends[j] = end

    def doc_at(n):
        doc = 0
        for j in range(blocks):
            doc = doc + (n >= ends[j]).astype(jnp.int32)
        return doc

    def block_at(n):
        doc = doc_at(n)
        block = 0
        for j in range(1, blocks):
            block = block + jnp.where(doc_ids[j] == doc, j, 0)
        return block

    stop = [ends[doc_ids[b]] for b in range(blocks)]
    start = [stop[b] - counts[doc_ids[b]] for b in range(blocks)]

    def has(b, first):
        return (start[b] < first + 4) & (stop[b] > first)

    def last(b, first):
        return jnp.clip(stop[b] - 1 - first, 0, 3)

    first = 4 * z
    rim = jnp.where(upper == 0, 0, 12)
    other = [jnp.where(upper == 0, (stop[b] > 8).astype(jnp.int32), (start[b] < 8).astype(jnp.int32)) == 1 for b in range(blocks)]
    page_block = [block_at(first + p) for p in range(4)]
    same = [None] + [doc_at(first + p) == doc_at(first + p - 1) for p in range(1, 4)]
    seam = jnp.where(upper == 0, 3, 11)
    seam_block = block_at(seam)
    seam_cut = doc_at(seam) == doc_at(seam + 1)
    mid_block = block_at(7)
    mid_cut = doc_at(7) == doc_at(8)

    def of(values, index):
        got = values[0]
        for n in range(1, blocks):
            got = jnp.where(index == n, values[n], got)
        return got

    def has_at(b, base):
        return (of(start, b) < base + 4) & (of(stop, b) > base)

    def last_at(b, base):
        return jnp.clip(of(stop, b) - 1 - base, 0, 3)

    def prepare(g):
        for n in range(GROUPS):
            @pl.when(g == n)
            def _():
                own[n].wait()
        part = raw.at[g, pl.ds(0, 3)]
        wait(part, q_rsem.at[g])
        value = raw[g].astype(jnp.float32).reshape(32, blocks, 512)
        value = jnp.swapaxes(value, 0, 1).astype(jnp.bfloat16)
        for n in range(4):
            blk[g * 4 + n] = value[:, :, n * 128:(n + 1) * 128]

    def wait_kv(v):
        for h in range(2):
            @pl.when(v == h * (STEPS // 2))
            def _():
                own[GROUPS + h].wait()
                wait(kv.at[h, pl.ds(0, 3)], kv_rsem.at[h])

    sub = lax.broadcasted_iota(jnp.int32, (8, 128), 0)

    def attend(v, question):
        h = v // (STEPS // 2)
        tile = jnp.zeros((8, 128), jnp.float32)
        top = total = mixed = None
        for p in range(4):
            s = lax.dot_general(
                question(p), kv[h, p, 0], (((1,), (1,)), ((), ())),
                preferred_element_type=jnp.float32,
            ) * HEAD_DIM ** (-0.5)
            t = jnp.max(s, axis=-1, keepdims=True)
            e = jnp.exp(s - t)
            n = jnp.sum(e, axis=-1, keepdims=True)
            o = jnp.dot(e.astype(jnp.bfloat16), kv[h, p, 1], preferred_element_type=jnp.float32)
            if p == 0:
                top, total, mixed = t, n, o
            else:
                before = jnp.where(same[p], top, FAR)
                top = jnp.maximum(before, t)
                a, b = jnp.exp(before - top), jnp.exp(t - top)
                total = a * total + b * n
                mixed = a * mixed + b * o
            run[v, p] = (mixed / total).astype(jnp.bfloat16)
            tile = jnp.where(sub == p, to_row(top + jnp.log(total), 0), tile)
        lse[v] = tile

    def finish(u, values):
        value = jnp.stack([x.astype(jnp.float32) for x in values], axis=0)
        fin[u] = jnp.swapaxes(value, 0, 1).astype(jnp.bfloat16)
        column = pl.ds(pl.multiple_of(mine * 2048 + u * 128, 128), 128)
        for k in range(1, 4):
            peer, i = plane(k)
            remote(fin.at[u, pl.ds(i * 8, 8)], out_hbm.at[:, :, column], o_ssem, o_rsem, peer)
        pltpu.make_async_copy(fin.at[u, pl.ds(mine * 8, 8)], out_hbm.at[:, :, column], o_own).start()

    @pl.when(leaf)
    def _():
        def pass_on(g):
            prepare(g)
            for n in range(4):
                c = g * 4 + n
                remote(blk.at[c], s1r.at[c], s_ssem, s_rsem.at[c], away)

        pass_on(0)
        has_own = [has(b, first) for b in range(blocks)]
        last_own = [last(b, first) for b in range(blocks)]
        seam_last = last_at(seam_block, first)

        @pl.loop(0, STEPS + LAG + 1)
        def _(t):
            @pl.when((t % 4 == 0) & (t < STEPS - 4))
            def _():
                pass_on(t // 4 + 1)

            @pl.when(t < STEPS)
            def _():
                wait_kv(t)
                wait(cr.at[t], c_rsem.at[t])
                attend(t, lambda p: jnp.concatenate([blk[t, page_block[p]], cr[t, p]], axis=0))
                remote(run.at[t, :, pl.ds(32, 96)], dr.at[t], d_ssem, d_rsem.at[t], away)
                remote(lse.at[t], dlr.at[t], dl_ssem, dl_rsem.at[t], away)

            @pl.when(t >= LAG + 1)
            def _():
                u = t - LAG - 1
                wait(fr.at[u], f_rsem.at[u])
                wait(flr.at[u], fl_rsem.at[u])
                near = to_col(pick([lse[u, p:p + 1] for p in range(4)], seam_last), 0, 32)
                far = to_col(flr[u, 0:1], 0, 32)
                whole = merge(
                    run[u, seam_last, 0:32], near,
                    of([fr[u, b] for b in range(blocks)], seam_block), far,
                )
                values = []
                for b in range(blocks):
                    value = jnp.where(has_own[b], run[u, last_own[b], 0:32], fr[u, b])
                    values.append(jnp.where(seam_cut & (seam_block == b), whole, value))
                finish(u, values)

        wait(blk, s_ssem)
        wait(dr, d_ssem)
        wait(dlr, dl_ssem)

    @pl.when(hub)
    def _():
        prepare(jnp.int32(0))
        has_rim = [has(b, rim) for b in range(blocks)]
        last_rim = [last(b, rim) for b in range(blocks)]
        has_own = [has(b, first) for b in range(blocks)]
        last_own = [last(b, first) for b in range(blocks)]
        rim_block = [block_at(rim + p) for p in range(4)]
        seam_rim, seam_own = last_at(seam_block, rim), last_at(seam_block, first)
        mid_rim, mid_own = last_at(mid_block, rim), last_at(mid_block, first)
        mid_has_rim = has_at(mid_block, rim)
        lane = lax.broadcasted_iota(jnp.int32, (1, 128), 1)

        def rows(ref, u):
            return [ref[u, p:p + 1] for p in range(4)]

        @pl.loop(0, rounds + 1)
        def _(t):
            @pl.when((t >= LAG) & (t < rounds))
            def _():
                w = t - LAG
                wait(dr.at[w], d_rsem.at[w])
                wait(dlr.at[w], dl_rsem.at[w])
                rim_o = [dr[w, p] for p in range(4)]
                whole = merge(
                    pick(rim_o, seam_rim), to_col(pick(rows(dlr, w), seam_rim), 32, 96),
                    run[w, seam_own, 32:128], to_col(pick(rows(lse, w), seam_own), 32, 96),
                )
                for b in range(blocks):
                    value = jnp.where(has_own[b], run[w, last_own[b], 32:128], pick(rim_o, last_rim[b]))
                    oh[w, b] = jnp.where(seam_cut & (seam_block == b), whole, value)
                near = pick(rows(lse, w), mid_own)
                far = jnp.where(mid_has_rim, pick(rows(dlr, w), mid_rim), FAR)
                lh[w] = jnp.broadcast_to(join(near, far), (8, 128))

            @pl.when(t < rounds)
            def _():
                w = jnp.maximum(t - LAG, 0)
                c = jnp.minimum(t, STEPS - 1)

                @pl.when((t % 4 == 0) & (t > 0) & (t < STEPS))
                def _():
                    prepare(t // 4)

                @pl.when(t < STEPS)
                def _():
                    wait(s1r.at[t], s_rsem.at[t])

                asks = t < STEPS
                for b in range(blocks):
                    ask = other[b] & asks
                    xs[t, b, 0:32] = jnp.where(ask, s1r[c, b], oh[w, b, 32:64])
                    xs[t, b, 32:64] = jnp.where(ask, blk[c, b], oh[w, b, 64:96])
                xs[t, blocks] = oh[w, mid_block, 32:96]
                xls[t] = lh[w]
                remote(xs.at[t], xr.at[t], x_ssem, x_rsem.at[t], across)
                remote(xls.at[t], xlr.at[t], xl_ssem, xl_rsem.at[t], across)

            @pl.when(t >= 1)
            def _():
                v = t - 1
                wait(xr.at[v], x_rsem.at[v])
                wait(xlr.at[v], xl_rsem.at[v])

                @pl.when(v < STEPS)
                def _():
                    for b in range(blocks):
                        qt[v, b, 0:32] = s1r[v, b]
                        qt[v, b, 32:64] = blk[v, b]
                        qt[v, b, 64:128] = xr[v, b]
                    for p in range(4):
                        cs[v, p] = qt[v, rim_block[p], 32:128]
                    remote(cs.at[v], cr.at[v], c_ssem, c_rsem.at[v], away)

                @pl.when(v >= LAG)
                def _():
                    u = v - LAG
                    near = jnp.where(lane < 32, pick(rows(lse, u), mid_own), lh[u, 0:1])
                    far = pltpu.roll(xlr[v, 0:1], 64, 1)
                    part = jnp.concatenate([run[u, mid_own, 0:32], oh[u, mid_block, 0:32]], axis=0)
                    whole = merge(part, to_col(near, 0, 64), xr[v, blocks], to_col(far, 0, 64))
                    values = []
                    for b in range(blocks):
                        cut = mid_cut & (mid_block == b)
                        leafs = jnp.where(other[b], xr[v, b, 0:32], run[u, last_own[b], 0:32])
                        hubs = jnp.where(other[b], xr[v, b, 32:64], oh[u, b, 0:32])
                        fs[u, b] = jnp.where(cut, whole[0:32], leafs)
                        values.append(jnp.where(cut, whole[32:64], hubs))
                    tail = pick(rows(lse, u), seam_own)
                    tail = jnp.where(mid_cut & (mid_block == seam_block), join(tail, far), tail)
                    fls[u] = jnp.broadcast_to(tail, (8, 128))
                    remote(fs.at[u], fr.at[u], f_ssem, f_rsem.at[u], away)
                    remote(fls.at[u], flr.at[u], fl_ssem, fl_rsem.at[u], away)
                    finish(u, values)

            @pl.when((t >= LAG - 1) & (t < STEPS + LAG - 1))
            def _():
                v = t - LAG + 1
                wait_kv(v)
                attend(v, lambda p: qt[v, page_block[p]])

        wait(xs, x_ssem)
        wait(xls, xl_ssem)
        wait(cs, c_ssem)
        wait(fs, f_ssem)
        wait(fls, fl_ssem)

    for g in range(GROUPS):
        wait(raw.at[g, pl.ds(0, 3)], q_ssem)
    for h in range(2):
        wait(kv.at[h, pl.ds(0, 3)], kv_ssem)
    theirs, ours = fin.at[:, pl.ds(0, 24)], fin.at[:, pl.ds(0, 8)]
    wait(theirs, o_ssem)
    wait(theirs, o_rsem)
    wait(ours, o_own)


def line_call(queries, kv_cache, page_counts, doc_ids):
    blocks = queries.shape[1]
    bf16, f32 = jnp.bfloat16, jnp.float32
    any_spec = pl.BlockSpec(memory_space=pl.ANY)
    smem_spec = pl.BlockSpec(memory_space=pltpu.SMEM)
    dma = pltpu.SemaphoreType.DMA
    rounds = STEPS + LAG
    tiles = pltpu.VMEM((STEPS, 8, 128), f32)
    mids = pltpu.VMEM((rounds, 8, 128), f32)
    pieces = pltpu.VMEM((STEPS, blocks, 32, 128), bf16)
    swaps = pltpu.VMEM((rounds, blocks + 1, 64, 128), bf16)
    quads = pltpu.VMEM((STEPS, 4, 96, 128), bf16)
    one, step, mid = dma(()), dma((STEPS,)), dma((rounds,))
    return pl.pallas_call(
        line_kernel,
        out_shape=jax.ShapeDtypeStruct(queries.shape, bf16),
        in_specs=[smem_spec, smem_spec, any_spec, any_spec],
        out_specs=any_spec,
        scratch_shapes=[
            pltpu.VMEM((GROUPS, 4, 8, blocks, 512), bf16),
            pltpu.VMEM((2, 4, 2, 512, 128), bf16),
            pieces, pieces, swaps, swaps, mids, mids,
            quads, quads, quads, tiles, pieces, pieces, tiles, tiles,
            pltpu.VMEM((STEPS, blocks, 128, 128), bf16),
            pltpu.VMEM((STEPS, 4, 128, 128), bf16),
            tiles,
            pltpu.VMEM((STEPS, blocks, 96, 128), bf16),
            tiles,
            pltpu.VMEM((STEPS, 32, blocks, 128), bf16),
            pltpu.SMEM((blocks,), jnp.int32),
            one, dma((GROUPS,)), dma((GROUPS,)), one, dma((2,)), dma((2,)),
            one, step, one, mid, one, mid,
            one, step, one, step, one, step, one, step, one, step,
            one, one, one,
        ],
        compiler_params=pltpu.CompilerParams(collective_id=1, has_side_effects=True),
    )(page_counts, doc_ids, queries, kv_cache)


def body(queries, kv_cache, page_counts, doc_ids):
    peers = lax.axis_size("ctx")
    rows, blocks, width = queries.shape
    if (peers, rows, blocks) == (16, 8, 8) and kv_cache.shape == (1, 2, 512, 1024):
        return line_call(queries, kv_cache, page_counts, doc_ids)
    assert kv_cache.shape[0] == 1 and width == 64 * HEAD_DIM
    wide = width // CHUNKS
    any_spec = pl.BlockSpec(memory_space=pl.ANY)
    smem_spec = pl.BlockSpec(memory_space=pltpu.SMEM)
    dma = pltpu.SemaphoreType.DMA
    pieces = pltpu.VMEM((CHUNKS, peers, rows, wide), jnp.bfloat16)
    stats = pltpu.VMEM((peers, rows, 128), jnp.float32)
    return pl.pallas_call(
        functools.partial(attend_kernel, peers),
        out_shape=jax.ShapeDtypeStruct(queries.shape, jnp.bfloat16),
        in_specs=[smem_spec, smem_spec, any_spec, any_spec],
        out_specs=any_spec,
        scratch_shapes=[
            pltpu.VMEM((CHUNKS, rows, blocks, wide), jnp.bfloat16),
            pltpu.VMEM((CHUNKS, blocks, rows, wide), jnp.bfloat16),
            pieces, pieces, pieces, pieces,
            stats, stats, stats, stats,
            pltpu.VMEM((peers, rows, wide), jnp.float32),
            pltpu.VMEM((CHUNKS, rows, blocks, wide), jnp.bfloat16),
            pltpu.VMEM(kv_cache.shape[1:], jnp.bfloat16),
            pltpu.SMEM((blocks,), jnp.int32),
            pltpu.SMEM((peers,), jnp.int32),
            pltpu.SMEM((peers,), jnp.int32),
            pltpu.SMEM((peers + 1,), jnp.int32),
            dma((CHUNKS,)),
            dma((CHUNKS,)), dma((CHUNKS,)), dma((CHUNKS,)), dma((CHUNKS,)),
            dma(()), dma(()), dma((CHUNKS,)), dma((CHUNKS,)), dma(()),
            dma(()), dma((CHUNKS,)),
        ],
        compiler_params=pltpu.CompilerParams(collective_id=0, has_side_effects=True),
    )(page_counts, doc_ids, queries, kv_cache)


def solution(mesh):
    placed = (
        P(("group", "ctx"), None, None),
        P(("group", "ctx"), None, None, None),
        P("group"),
        P("group"),
    )
    return jax.shard_map(
        body, mesh=mesh, in_specs=placed, out_specs=P(("group", "ctx"), None, None), check_vma=False
    )
```

```python
import functools

import jax
import jax.numpy as jnp
from jax import lax
from jax.experimental import pallas as pl
from jax.experimental.pallas import tpu as pltpu
from jax.sharding import PartitionSpec as P

HEAD_DIM = 128
CHUNKS = 4


def attend_kernel(
    peers, counts, doc_ids, q_hbm, kv_hbm, out_hbm,
    raw_buf, doc_buf, send_buf, q_buf, o_buf, got_buf, s_buf, stats_buf, w_buf, top_buf,
    run_buf, out_buf, kv_buf, ends, page_doc, page_block, fresh,
    raw_sem, q_send, q_recv, o_send, o_recv, s_send, s_recv, own_q_sem, own_o_sem, own_s_sem,
    kv_sem, out_sem,
):
    chunks, _, rows, wide = q_buf.shape
    blocks = counts.shape[0]
    me = lax.axis_index("ctx")
    tokens = peers * rows
    heads_chunk = wide // HEAD_DIM
    kv_heads = kv_buf.shape[2] // HEAD_DIM
    groups = chunks * heads_chunk // kv_heads
    mesh_id = pl.DeviceIdType.MESH

    barrier = pltpu.get_barrier_semaphore()

    @pl.loop(1, peers)
    def _(k):
        pl.semaphore_signal(
            barrier, inc=1, device_id={"ctx": lax.rem(me + k, peers)}, device_id_type=mesh_id
        )

    def columns(c):
        return pl.ds(c * wide, wide)

    raw_copies = [
        pltpu.make_async_copy(q_hbm.at[:, :, columns(c)], raw_buf.at[c], raw_sem.at[c])
        for c in range(chunks)
    ]
    for copy in raw_copies:
        copy.start()
    kv_copy = pltpu.make_async_copy(kv_hbm.at[0], kv_buf, kv_sem)
    kv_copy.start()

    end = 0
    for j in range(blocks):
        end = end + counts[j]
        ends[j] = end

    def locate(n, before):
        doc = 0
        for j in range(blocks):
            doc = doc + (n >= ends[j]).astype(jnp.int32)
        block = 0
        for j in range(1, blocks):
            block = block + jnp.where(doc_ids[j] == doc, j, 0)
        page_doc[n] = doc
        page_block[n] = block
        fresh[n] = (doc != before).astype(jnp.int32)
        return doc

    lax.fori_loop(0, peers, locate, jnp.int32(-1))
    fresh[peers] = 1

    def send(src, dst, send_sem, recv_sem):
        @pl.loop(1, peers)
        def _(k):
            peer = lax.rem(me + k, peers)
            pltpu.make_async_remote_copy(
                src_ref=src.at[peer], dst_ref=dst.at[me], send_sem=send_sem,
                recv_sem=recv_sem, device_id={"ctx": peer}, device_id_type=mesh_id,
            ).start()

    def drain(ref, sem):
        part = ref.at[pl.ds(0, peers - 1)]
        pltpu.make_async_copy(part, part, sem).wait()

    own_q, own_o = [], []
    for c in range(chunks):
        raw_copies[c].wait()
        raw = raw_buf[c].astype(jnp.float32)
        doc_buf[c] = jnp.swapaxes(raw, 0, 1).astype(jnp.bfloat16)

        @pl.loop(0, peers)
        def _(n):
            send_buf[c, n] = doc_buf[c, page_block[n]]

        if c == 0:
            pl.semaphore_wait(barrier, peers - 1)
        send(send_buf.at[c], q_buf.at[c], q_send.at[c], q_recv.at[c])
        copy = pltpu.make_async_copy(send_buf.at[c, me], q_buf.at[c, me], own_q_sem.at[c])
        copy.start()
        own_q.append(copy)

    s_buf[...] = jnp.zeros_like(s_buf)
    kv_copy.wait()
    lane = lax.broadcasted_iota(jnp.int32, (tokens, 128), 1)
    own_s = pltpu.make_async_copy(s_buf.at[me], stats_buf.at[me], own_s_sem)
    for c in range(chunks):
        own_q[c].wait()
        drain(q_buf.at[c], q_recv.at[c])

        def head(j, carry):
            lanes = pl.ds(pl.multiple_of(j * HEAD_DIM, HEAD_DIM), HEAD_DIM)
            h = c * heads_chunk + j
            kv_lanes = pl.ds(pl.multiple_of(h // groups * HEAD_DIM, HEAD_DIM), HEAD_DIM)
            q = q_buf[c, :, :, lanes].astype(jnp.float32).reshape(tokens, HEAD_DIM)
            s = lax.dot_general(
                q.astype(jnp.bfloat16), kv_buf[0, :, kv_lanes], (((1,), (1,)), ((), ())),
                preferred_element_type=jnp.float32,
            ) * HEAD_DIM ** (-0.5)
            top = jnp.max(s, axis=-1, keepdims=True)
            p = jnp.exp(s - top)
            total = jnp.sum(p, axis=-1, keepdims=True)
            o = jnp.dot(
                p.astype(jnp.bfloat16), kv_buf[1, :, kv_lanes],
                preferred_element_type=jnp.float32,
            ) / total
            o_buf[c, :, :, lanes] = o.reshape(peers, rows, HEAD_DIM).astype(jnp.bfloat16)
            old = s_buf[...].reshape(tokens, 128)
            new = jnp.where(lane == h, top, jnp.where(lane == h + 64, total, old))
            s_buf[...] = new.reshape(peers, rows, 128)
            return carry

        lax.fori_loop(0, heads_chunk, head, 0)
        if c == chunks - 1:
            send(s_buf, stats_buf, s_send, s_recv)
            own_s.start()
        send(o_buf.at[c], got_buf.at[c], o_send.at[c], o_recv.at[c])
        copy = pltpu.make_async_copy(o_buf.at[c, me], got_buf.at[c, me], own_o_sem.at[c])
        copy.start()
        own_o.append(copy)

    own_s.wait()
    drain(stats_buf, s_recv)

    def forward(n, top):
        mine = stats_buf[n]
        top = jnp.where(fresh[n] == 1, mine, jnp.maximum(top, mine))
        top_buf[n] = top
        return top

    def backward(i, top):
        n = peers - 1 - i
        top = jnp.where(fresh[n + 1] == 1, top_buf[n], top)
        top_buf[n] = top
        return top

    def weigh(n, total):
        mine = stats_buf[n]
        w = jnp.exp(mine - top_buf[n]) * pltpu.roll(mine, 128 - 64, 1)
        w_buf[n] = w
        total = jnp.where(fresh[n] == 1, w, total + w)
        top_buf[n] = total
        return total

    def norm(i, total):
        n = peers - 1 - i
        total = jnp.where(fresh[n + 1] == 1, top_buf[n], total)
        w_buf[n] = w_buf[n] / total
        return total

    zero = jnp.zeros((rows, 128), jnp.float32)
    lax.fori_loop(0, peers, forward, zero)
    lax.fori_loop(0, peers, backward, zero)
    lax.fori_loop(0, peers, weigh, zero)
    lax.fori_loop(0, peers, norm, zero)

    outs = []
    for c in range(chunks):
        own_o[c].wait()
        drain(got_buf.at[c], o_recv.at[c])

        def visit(n, acc):
            w = w_buf[n]
            w = jnp.concatenate(
                [
                    jnp.broadcast_to(w[:, h:h + 1], (rows, HEAD_DIM))
                    for h in range(c * heads_chunk, (c + 1) * heads_chunk)
                ],
                axis=1,
            )
            mine = w * got_buf[c, n].astype(jnp.float32)
            acc = jnp.where(fresh[n] == 1, mine, acc + mine)
            run_buf[n] = acc
            return acc

        lax.fori_loop(0, peers, visit, jnp.zeros((rows, wide), jnp.float32), unroll=2)
        picked = jnp.stack([run_buf[jnp.clip(ends[doc_ids[b]] - 1, 0, peers - 1)] for b in range(blocks)], axis=0)
        out_buf[c] = jnp.swapaxes(picked, 0, 1).astype(jnp.bfloat16)
        copy = pltpu.make_async_copy(out_buf.at[c], out_hbm.at[:, :, columns(c)], out_sem.at[c])
        copy.start()
        outs.append(copy)
    drain(s_buf, s_send)
    for c in range(chunks):
        drain(send_buf.at[c], q_send.at[c])
        drain(o_buf.at[c], o_send.at[c])
        outs[c].wait()


STEPS = 16
LAG = 6
BACK = 2
GROUPS = 8
AHEAD = 4
FAR = -1e30


def merge(o1, l1, o2, l2):
    top = jnp.maximum(l1, l2)
    w1, w2 = jnp.exp(l1 - top), jnp.exp(l2 - top)
    out = (w1 * o1.astype(jnp.float32) + w2 * o2.astype(jnp.float32)) / (w1 + w2)
    return out.astype(jnp.bfloat16)


def join(l1, l2):
    top = jnp.maximum(l1, l2)
    return top + jnp.log(jnp.exp(l1 - top) + jnp.exp(l2 - top))


def to_row(col, first):
    shape = (col.shape[0], 128)
    hit = lax.broadcasted_iota(jnp.int32, shape, 1) == lax.broadcasted_iota(jnp.int32, shape, 0) + first
    return jnp.sum(jnp.where(hit, col, 0.0), axis=0, keepdims=True)


def to_col(row, first, count):
    shape = (count, 128)
    hit = lax.broadcasted_iota(jnp.int32, shape, 1) == lax.broadcasted_iota(jnp.int32, shape, 0) + first
    return jnp.sum(jnp.where(hit, row, 0.0), axis=1, keepdims=True)


def pick(parts, index):
    got = parts[0]
    for n in range(1, len(parts)):
        got = jnp.where(index == n, parts[n], got)
    return got


def line_kernel(
    counts, doc_ids, q_hbm, kv_hbm, out_hbm,
    raw, kv, blk, s1r, xs, xr, xls, xlr, cs, cr, dr, dlr, fs, fr, fls, flr,
    qt, run, lse, oh, lh, fin, turn, done, ends,
    q_ssem, q_rsem, q_own, kv_ssem, kv_rsem, kv_own, s_ssem, s_rsem, x_ssem, x_rsem, xl_ssem, xl_rsem,
    c_ssem, c_rsem, d_ssem, d_rsem, dl_ssem, dl_rsem, f_ssem, f_rsem, fl_ssem, fl_rsem,
    o_ssem, o_rsem, o_own,
):
    blocks = counts.shape[0]
    rounds = STEPS + LAG
    me = lax.axis_index("ctx")
    z, mine = me // 4, me % 4
    upper = z // 2
    hub = (z == 1) | (z == 2)
    leaf = (z == 0) | (z == 3)
    away = jnp.where((z == 0) | (z == 2), me + 4, me - 4)
    across = jnp.where(z == 1, me + 4, me - 4)
    mesh_id = pl.DeviceIdType.MESH

    def plane(k):
        return z * 4 + (mine + k) % 4, (mine + k) % 4

    barrier = pltpu.get_barrier_semaphore()
    for k in range(1, 4):
        pl.semaphore_signal(barrier, inc=1, device_id={"ctx": plane(k)[0]}, device_id_type=mesh_id)
    pl.semaphore_signal(barrier, inc=1, device_id={"ctx": away}, device_id_type=mesh_id)

    @pl.when(hub)
    def _():
        pl.semaphore_signal(barrier, inc=1, device_id={"ctx": across}, device_id_type=mesh_id)

    def lanes(i, g):
        return pl.ds(pl.multiple_of(i * 2048 + g * 256, 128), 256)

    def heads(i, h):
        return pl.ds(pl.multiple_of(i * 256 + h * 128, 128), 128)

    for g in range(GROUPS):
        pltpu.make_async_copy(q_hbm.at[:, :, lanes(mine, g)], raw.at[g, mine], q_own.at[g]).start()
    for h in range(2):
        pltpu.make_async_copy(kv_hbm.at[0, :, :, heads(mine, h)], kv.at[h, mine], kv_own.at[h]).start()

    def remote(src, dst, ssem, rsem, peer):
        pltpu.make_async_remote_copy(
            src_ref=src, dst_ref=dst, send_sem=ssem, recv_sem=rsem,
            device_id={"ctx": peer}, device_id_type=mesh_id,
        ).start()

    def wait(ref, sem):
        pltpu.make_async_copy(ref, ref, sem).wait()

    @pl.when(hub)
    def _():
        pl.semaphore_wait(barrier, 5)

    @pl.when(leaf)
    def _():
        pl.semaphore_wait(barrier, 4)

    def send_group(g):
        for k in range(1, 4):
            peer, i = plane(k)
            remote(q_hbm.at[:, :, lanes(i, g)], raw.at[g, mine], q_ssem, q_rsem.at[g], peer)

    def send_kv(h):
        for k in range(1, 4):
            peer, i = plane(k)
            remote(kv_hbm.at[0, :, :, heads(i, h)], kv.at[h, mine], kv_ssem, kv_rsem.at[h], peer)

    for g in range(AHEAD):
        send_group(g)
    send_kv(0)
    for g in range(AHEAD, GROUPS):
        send_group(g)
    send_kv(1)

    end = 0
    for j in range(blocks):
        end = end + counts[j]
        ends[j] = end

    def doc_at(n):
        doc = 0
        for j in range(blocks):
            doc = doc + (n >= ends[j]).astype(jnp.int32)
        return jnp.minimum(doc, blocks - 1)

    stop = [ends[j] for j in range(blocks)]
    start = [stop[j] - counts[j] for j in range(blocks)]
    doc_block = []
    for j in range(blocks):
        block = 0
        for b in range(1, blocks):
            block = block + jnp.where(doc_ids[b] == j, b, 0)
        doc_block.append(jnp.minimum(block, blocks - 1))

    def has(j, first):
        return (start[j] < first + 4) & (stop[j] > first)

    def last(j, first):
        return jnp.clip(stop[j] - 1 - first, 0, 3)

    def has_at(j, first):
        return (ends[j] - counts[j] < first + 4) & (ends[j] > first)

    def last_at(j, first):
        return jnp.clip(ends[j] - 1 - first, 0, 3)

    first = 4 * z
    rim = jnp.where(upper == 0, 0, 12)
    other = [jnp.where(upper == 0, (stop[j] > 8).astype(jnp.int32), (start[j] < 8).astype(jnp.int32)) == 1 for j in range(blocks)]
    page_doc = [doc_at(first + p) for p in range(4)]
    same = [None] + [page_doc[p] == page_doc[p - 1] for p in range(1, 4)]
    seam = jnp.where(upper == 0, 3, 11)
    seam_doc, mid_doc = doc_at(seam), doc_at(7)
    seam_cut = seam_doc == doc_at(seam + 1)
    mid_cut = mid_doc == doc_at(8)

    def prepare(g):
        wait(raw.at[g, mine], q_own.at[g])
        wait(raw.at[g, pl.ds(0, 3)], q_rsem.at[g])
        value = raw[g].astype(jnp.float32).reshape(32, blocks, 256)
        turn[...] = jnp.swapaxes(value, 0, 1).astype(jnp.bfloat16)
        for j in range(blocks):
            value = turn[doc_block[j]]
            blk[g * 2, j] = value[:, 0:128]
            blk[g * 2 + 1, j] = value[:, 128:256]

    def wait_kv(v):
        for h in range(2):
            @pl.when(v == h * (STEPS // 2))
            def _():
                wait(kv.at[h, mine], kv_own.at[h])
                wait(kv.at[h, pl.ds(0, 3)], kv_rsem.at[h])

    sub = lax.broadcasted_iota(jnp.int32, (8, 128), 0)

    def attend(v, question):
        h = v // (STEPS // 2)
        tile = jnp.zeros((8, 128), jnp.float32)
        top = total = mixed = None
        for p in range(4):
            s = lax.dot_general(
                question(p), kv[h, p, 0], (((1,), (1,)), ((), ())),
                preferred_element_type=jnp.float32,
            ) * HEAD_DIM ** (-0.5)
            t = jnp.max(s, axis=-1, keepdims=True)
            e = jnp.exp(s - t)
            n = jnp.sum(e, axis=-1, keepdims=True)
            o = jnp.dot(e.astype(jnp.bfloat16), kv[h, p, 1], preferred_element_type=jnp.float32)
            if p == 0:
                top, total, mixed = t, n, o
            else:
                before = jnp.where(same[p], top, FAR)
                top = jnp.maximum(before, t)
                a, b = jnp.exp(before - top), jnp.exp(t - top)
                total = a * total + b * n
                mixed = a * mixed + b * o
            run[v, p] = (mixed / total).astype(jnp.bfloat16)
            tile = jnp.where(sub == p, to_row(top + jnp.log(total), 0), tile)
        lse[v] = tile

    def finish(u, values):
        for j in range(blocks):
            done[j] = values[j]
        value = jnp.stack([done[doc_ids[b]].astype(jnp.float32) for b in range(blocks)], axis=0)
        fin[u] = jnp.swapaxes(value, 0, 1).astype(jnp.bfloat16)
        column = pl.ds(pl.multiple_of(mine * 2048 + u * 128, 128), 128)
        for k in range(1, 4):
            peer, i = plane(k)
            remote(fin.at[u, pl.ds(i * 8, 8)], out_hbm.at[:, :, column], o_ssem, o_rsem, peer)
        pltpu.make_async_copy(fin.at[u, pl.ds(mine * 8, 8)], out_hbm.at[:, :, column], o_own).start()

    @pl.when(leaf)
    def _():
        def pass_on(g):
            prepare(g)
            for n in range(2):
                c = g * 2 + n
                remote(blk.at[c], s1r.at[c], s_ssem, s_rsem.at[c], away)

        for g in range(AHEAD):
            pass_on(g)
        has_own = [has(j, first) for j in range(blocks)]
        last_own = [last(j, first) for j in range(blocks)]
        seam_last = last_at(seam_doc, first)

        @pl.loop(0, STEPS + LAG + 1)
        def _(t):
            @pl.when(t < STEPS)
            def _():
                wait_kv(t)
                wait(cr.at[t], c_rsem.at[t])
                attend(t, lambda p: jnp.concatenate([blk[t, page_doc[p]], cr[t, p]], axis=0))
                remote(run.at[t, :, pl.ds(32, 96)], dr.at[t], d_ssem, d_rsem.at[t], away)
                remote(lse.at[t], dlr.at[t], dl_ssem, dl_rsem.at[t], away)

            @pl.when((t % 2 == 0) & (t < (GROUPS - AHEAD) * 2))
            def _():
                pass_on(t // 2 + AHEAD)

            @pl.when(t >= LAG + 1)
            def _():
                u = t - LAG - 1
                wait(fr.at[u], f_rsem.at[u])
                wait(flr.at[u], fl_rsem.at[u])
                near = to_col(pick([lse[u, p:p + 1] for p in range(4)], seam_last), 0, 32)
                far = to_col(flr[u, 0:1], 0, 32)
                theirs = [fr[u, j] for j in range(blocks)]
                whole = merge(run[u, seam_last, 0:32], near, pick(theirs, seam_doc), far)
                values = []
                for j in range(blocks):
                    value = jnp.where(has_own[j], run[u, last_own[j], 0:32], theirs[j])
                    values.append(jnp.where(seam_cut & (seam_doc == j), whole, value))
                finish(u, values)

        wait(blk, s_ssem)
        wait(dr, d_ssem)
        wait(dlr, dl_ssem)

    @pl.when(hub)
    def _():
        last_rim = [last(b, rim) for b in range(blocks)]
        has_own = [has(b, first) for b in range(blocks)]
        last_own = [last(b, first) for b in range(blocks)]
        rim_doc = [doc_at(rim + p) for p in range(4)]
        seam_rim, seam_own = last_at(seam_doc, rim), last_at(seam_doc, first)
        mid_rim, mid_own = last_at(mid_doc, rim), last_at(mid_doc, first)
        mid_has_rim = has_at(mid_doc, rim)
        lane = lax.broadcasted_iota(jnp.int32, (1, 128), 1)

        def rows(ref, u):
            return [ref[u, p:p + 1] for p in range(4)]

        @pl.loop(0, rounds + BACK)
        def _(t):
            @pl.when((t >= LAG) & (t < rounds))
            def _():
                w = t - LAG
                wait(dr.at[w], d_rsem.at[w])
                wait(dlr.at[w], dl_rsem.at[w])
                rim_o = [dr[w, p] for p in range(4)]
                whole = merge(
                    pick(rim_o, seam_rim), to_col(pick(rows(dlr, w), seam_rim), 32, 96),
                    run[w, seam_own, 32:128], to_col(pick(rows(lse, w), seam_own), 32, 96),
                )
                for b in range(blocks):
                    value = jnp.where(has_own[b], run[w, last_own[b], 32:128], pick(rim_o, last_rim[b]))
                    oh[w, b] = jnp.where(seam_cut & (seam_doc == b), whole, value)
                near = pick(rows(lse, w), mid_own)
                far = jnp.where(mid_has_rim, pick(rows(dlr, w), mid_rim), FAR)
                lh[w] = jnp.broadcast_to(join(near, far), (8, 128))

            @pl.when(t < rounds)
            def _():
                w = jnp.maximum(t - LAG, 0)
                c = jnp.minimum(t, STEPS - 1)

                @pl.when((t % 2 == 0) & (t < STEPS))
                def _():
                    prepare(t // 2)

                @pl.when(t < STEPS)
                def _():
                    wait(s1r.at[t], s_rsem.at[t])

                asks = t < STEPS
                for b in range(blocks):
                    ask = other[b] & asks
                    xs[t, b, 0:32] = jnp.where(ask, s1r[c, b], oh[w, b, 32:64])
                    xs[t, b, 32:64] = jnp.where(ask, blk[c, b], oh[w, b, 64:96])
                @pl.when(t < LAG)
                def _():
                    part = pl.ds(1 - upper, blocks - 1)
                    remote(xs.at[t, part], xr.at[t, part], x_ssem, x_rsem.at[t], across)

                @pl.when((t >= LAG) & asks)
                def _():
                    xs[t, blocks] = oh[w, mid_doc, 32:96]
                    remote(xs.at[t], xr.at[t], x_ssem, x_rsem.at[t], across)

                @pl.when(t >= STEPS)
                def _():
                    part = pl.ds(upper, blocks - 1)
                    remote(xs.at[t, part], xr.at[t, part], x_ssem, x_rsem.at[t], across)

                @pl.when(t >= LAG)
                def _():
                    xls[t] = lh[w]
                    remote(xls.at[t], xlr.at[t], xl_ssem, xl_rsem.at[t], across)

            @pl.when(t >= BACK)
            def _():
                v = t - BACK
                inner = (v >= LAG) & (v < STEPS)

                @pl.when(inner)
                def _():
                    wait(xr.at[v], x_rsem.at[v])

                @pl.when(jnp.logical_not(inner))
                def _():
                    wait(xr.at[v, pl.ds(0, blocks - 1)], x_rsem.at[v])

                @pl.when(v < STEPS)
                def _():
                    for b in range(blocks):
                        qt[v, b, 0:32] = s1r[v, b]
                        qt[v, b, 32:64] = blk[v, b]
                        qt[v, b, 64:128] = xr[v, b]
                    for p in range(4):
                        cs[v, p] = qt[v, rim_doc[p], 32:128]
                    remote(cs.at[v], cr.at[v], c_ssem, c_rsem.at[v], away)

                @pl.when(v >= LAG)
                def _():
                    u = v - LAG
                    wait(xlr.at[v], xl_rsem.at[v])
                    near = jnp.where(lane < 32, pick(rows(lse, u), mid_own), lh[u, 0:1])
                    far = pltpu.roll(xlr[v, 0:1], 64, 1)
                    part = jnp.concatenate([run[u, mid_own, 0:32], oh[u, mid_doc, 0:32]], axis=0)
                    theirs = pick([xr[v, j] for j in range(blocks)], mid_doc)
                    theirs = jnp.where(v < STEPS, xr[v, blocks], theirs)
                    whole = merge(part, to_col(near, 0, 64), theirs, to_col(far, 0, 64))
                    values = []
                    for b in range(blocks):
                        cut = mid_cut & (mid_doc == b)
                        leafs = jnp.where(other[b], xr[v, b, 0:32], run[u, last_own[b], 0:32])
                        hubs = jnp.where(other[b], xr[v, b, 32:64], oh[u, b, 0:32])
                        fs[u, b] = jnp.where(cut, whole[0:32], leafs)
                        values.append(jnp.where(cut, whole[32:64], hubs))
                    tail = pick(rows(lse, u), seam_own)
                    tail = jnp.where(mid_cut & (mid_doc == seam_doc), join(tail, far), tail)
                    fls[u] = jnp.broadcast_to(tail, (8, 128))
                    remote(fs.at[u], fr.at[u], f_ssem, f_rsem.at[u], away)
                    remote(fls.at[u], flr.at[u], fl_ssem, fl_rsem.at[u], away)
                    finish(u, values)

            @pl.when((t >= LAG - 1) & (t < STEPS + LAG - 1))
            def _():
                v = t - LAG + 1
                wait_kv(v)
                attend(v, lambda p: qt[v, page_doc[p]])

        wait(xs.at[pl.ds(LAG, STEPS - LAG)], x_ssem)
        for t in range(0, rounds, STEPS):
            wait(xs.at[pl.ds(t, LAG), pl.ds(0, blocks - 1)], x_ssem)
        wait(xls.at[pl.ds(LAG, STEPS)], xl_ssem)
        wait(cs, c_ssem)
        wait(fs, f_ssem)
        wait(fls, fl_ssem)

    for g in range(GROUPS):
        wait(raw.at[g, pl.ds(0, 3)], q_ssem)
    for h in range(2):
        wait(kv.at[h, pl.ds(0, 3)], kv_ssem)
    theirs, ours = fin.at[:, pl.ds(0, 24)], fin.at[:, pl.ds(0, 8)]
    wait(theirs, o_ssem)
    wait(theirs, o_rsem)
    wait(ours, o_own)


def line_call(queries, kv_cache, page_counts, doc_ids):
    blocks = queries.shape[1]
    bf16, f32 = jnp.bfloat16, jnp.float32
    any_spec = pl.BlockSpec(memory_space=pl.ANY)
    smem_spec = pl.BlockSpec(memory_space=pltpu.SMEM)
    dma = pltpu.SemaphoreType.DMA
    rounds = STEPS + LAG
    tiles = pltpu.VMEM((STEPS, 8, 128), f32)
    mids = pltpu.VMEM((rounds, 8, 128), f32)
    pieces = pltpu.VMEM((STEPS, blocks, 32, 128), bf16)
    swaps = pltpu.VMEM((rounds, blocks + 1, 64, 128), bf16)
    quads = pltpu.VMEM((STEPS, 4, 96, 128), bf16)
    one, step, mid = dma(()), dma((STEPS,)), dma((rounds,))
    return pl.pallas_call(
        line_kernel,
        out_shape=jax.ShapeDtypeStruct(queries.shape, bf16),
        in_specs=[smem_spec, smem_spec, any_spec, any_spec],
        out_specs=any_spec,
        scratch_shapes=[
            pltpu.VMEM((GROUPS, 4, 8, blocks, 256), bf16),
            pltpu.VMEM((2, 4, 2, 512, 128), bf16),
            pieces, pieces, swaps, swaps, mids, mids,
            quads, quads, quads, tiles, pieces, pieces, tiles, tiles,
            pltpu.VMEM((STEPS, blocks, 128, 128), bf16),
            pltpu.VMEM((STEPS, 4, 128, 128), bf16),
            tiles,
            pltpu.VMEM((STEPS, blocks, 96, 128), bf16),
            tiles,
            pltpu.VMEM((STEPS, 32, blocks, 128), bf16),
            pltpu.VMEM((blocks, 32, 256), bf16),
            pltpu.VMEM((blocks, 32, 128), bf16),
            pltpu.SMEM((blocks,), jnp.int32),
            one, dma((GROUPS,)), dma((GROUPS,)), one, dma((2,)), dma((2,)),
            one, step, one, mid, one, mid,
            one, step, one, step, one, step, one, step, one, step,
            one, one, one,
        ],
        compiler_params=pltpu.CompilerParams(collective_id=1, has_side_effects=True),
    )(page_counts, doc_ids, queries, kv_cache)


def body(queries, kv_cache, page_counts, doc_ids):
    peers = lax.axis_size("ctx")
    rows, blocks, width = queries.shape
    if (peers, rows, blocks) == (16, 8, 8) and kv_cache.shape == (1, 2, 512, 1024):
        return line_call(queries, kv_cache, page_counts, doc_ids)
    assert kv_cache.shape[0] == 1 and width == 64 * HEAD_DIM
    wide = width // CHUNKS
    any_spec = pl.BlockSpec(memory_space=pl.ANY)
    smem_spec = pl.BlockSpec(memory_space=pltpu.SMEM)
    dma = pltpu.SemaphoreType.DMA
    pieces = pltpu.VMEM((CHUNKS, peers, rows, wide), jnp.bfloat16)
    stats = pltpu.VMEM((peers, rows, 128), jnp.float32)
    return pl.pallas_call(
        functools.partial(attend_kernel, peers),
        out_shape=jax.ShapeDtypeStruct(queries.shape, jnp.bfloat16),
        in_specs=[smem_spec, smem_spec, any_spec, any_spec],
        out_specs=any_spec,
        scratch_shapes=[
            pltpu.VMEM((CHUNKS, rows, blocks, wide), jnp.bfloat16),
            pltpu.VMEM((CHUNKS, blocks, rows, wide), jnp.bfloat16),
            pieces, pieces, pieces, pieces,
            stats, stats, stats, stats,
            pltpu.VMEM((peers, rows, wide), jnp.float32),
            pltpu.VMEM((CHUNKS, rows, blocks, wide), jnp.bfloat16),
            pltpu.VMEM(kv_cache.shape[1:], jnp.bfloat16),
            pltpu.SMEM((blocks,), jnp.int32),
            pltpu.SMEM((peers,), jnp.int32),
            pltpu.SMEM((peers,), jnp.int32),
            pltpu.SMEM((peers + 1,), jnp.int32),
            dma((CHUNKS,)),
            dma((CHUNKS,)), dma((CHUNKS,)), dma((CHUNKS,)), dma((CHUNKS,)),
            dma(()), dma(()), dma((CHUNKS,)), dma((CHUNKS,)), dma(()),
            dma(()), dma((CHUNKS,)),
        ],
        compiler_params=pltpu.CompilerParams(collective_id=0, has_side_effects=True),
    )(page_counts, doc_ids, queries, kv_cache)


def solution(mesh):
    placed = (
        P(("group", "ctx"), None, None),
        P(("group", "ctx"), None, None, None),
        P("group"),
        P("group"),
    )
    return jax.shard_map(
        body, mesh=mesh, in_specs=placed, out_specs=P(("group", "ctx"), None, None), check_vma=False
    )
```

```python
import functools

import jax
import jax.numpy as jnp
from jax import lax
from jax.experimental import pallas as pl
from jax.experimental.pallas import tpu as pltpu
from jax.sharding import PartitionSpec as P

HEAD_DIM = 128
CHUNKS = 4


def attend_kernel(
    peers, counts, doc_ids, q_hbm, kv_hbm, out_hbm,
    raw_buf, doc_buf, send_buf, q_buf, o_buf, got_buf, s_buf, stats_buf, w_buf, top_buf,
    run_buf, out_buf, kv_buf, ends, page_doc, page_block, fresh,
    raw_sem, q_send, q_recv, o_send, o_recv, s_send, s_recv, own_q_sem, own_o_sem, own_s_sem,
    kv_sem, out_sem,
):
    chunks, _, rows, wide = q_buf.shape
    blocks = counts.shape[0]
    me = lax.axis_index("ctx")
    tokens = peers * rows
    heads_chunk = wide // HEAD_DIM
    kv_heads = kv_buf.shape[2] // HEAD_DIM
    groups = chunks * heads_chunk // kv_heads
    mesh_id = pl.DeviceIdType.MESH

    barrier = pltpu.get_barrier_semaphore()

    @pl.loop(1, peers)
    def _(k):
        pl.semaphore_signal(
            barrier, inc=1, device_id={"ctx": lax.rem(me + k, peers)}, device_id_type=mesh_id
        )

    def columns(c):
        return pl.ds(c * wide, wide)

    raw_copies = [
        pltpu.make_async_copy(q_hbm.at[:, :, columns(c)], raw_buf.at[c], raw_sem.at[c])
        for c in range(chunks)
    ]
    for copy in raw_copies:
        copy.start()
    kv_copy = pltpu.make_async_copy(kv_hbm.at[0], kv_buf, kv_sem)
    kv_copy.start()

    end = 0
    for j in range(blocks):
        end = end + counts[j]
        ends[j] = end

    def locate(n, before):
        doc = 0
        for j in range(blocks):
            doc = doc + (n >= ends[j]).astype(jnp.int32)
        block = 0
        for j in range(1, blocks):
            block = block + jnp.where(doc_ids[j] == doc, j, 0)
        page_doc[n] = doc
        page_block[n] = block
        fresh[n] = (doc != before).astype(jnp.int32)
        return doc

    lax.fori_loop(0, peers, locate, jnp.int32(-1))
    fresh[peers] = 1

    def send(src, dst, send_sem, recv_sem):
        @pl.loop(1, peers)
        def _(k):
            peer = lax.rem(me + k, peers)
            pltpu.make_async_remote_copy(
                src_ref=src.at[peer], dst_ref=dst.at[me], send_sem=send_sem,
                recv_sem=recv_sem, device_id={"ctx": peer}, device_id_type=mesh_id,
            ).start()

    def drain(ref, sem):
        part = ref.at[pl.ds(0, peers - 1)]
        pltpu.make_async_copy(part, part, sem).wait()

    own_q, own_o = [], []
    for c in range(chunks):
        raw_copies[c].wait()
        raw = raw_buf[c].astype(jnp.float32)
        doc_buf[c] = jnp.swapaxes(raw, 0, 1).astype(jnp.bfloat16)

        @pl.loop(0, peers)
        def _(n):
            send_buf[c, n] = doc_buf[c, page_block[n]]

        if c == 0:
            pl.semaphore_wait(barrier, peers - 1)
        send(send_buf.at[c], q_buf.at[c], q_send.at[c], q_recv.at[c])
        copy = pltpu.make_async_copy(send_buf.at[c, me], q_buf.at[c, me], own_q_sem.at[c])
        copy.start()
        own_q.append(copy)

    s_buf[...] = jnp.zeros_like(s_buf)
    kv_copy.wait()
    lane = lax.broadcasted_iota(jnp.int32, (tokens, 128), 1)
    own_s = pltpu.make_async_copy(s_buf.at[me], stats_buf.at[me], own_s_sem)
    for c in range(chunks):
        own_q[c].wait()
        drain(q_buf.at[c], q_recv.at[c])

        def head(j, carry):
            lanes = pl.ds(pl.multiple_of(j * HEAD_DIM, HEAD_DIM), HEAD_DIM)
            h = c * heads_chunk + j
            kv_lanes = pl.ds(pl.multiple_of(h // groups * HEAD_DIM, HEAD_DIM), HEAD_DIM)
            q = q_buf[c, :, :, lanes].astype(jnp.float32).reshape(tokens, HEAD_DIM)
            s = lax.dot_general(
                q.astype(jnp.bfloat16), kv_buf[0, :, kv_lanes], (((1,), (1,)), ((), ())),
                preferred_element_type=jnp.float32,
            ) * HEAD_DIM ** (-0.5)
            top = jnp.max(s, axis=-1, keepdims=True)
            p = jnp.exp(s - top)
            total = jnp.sum(p, axis=-1, keepdims=True)
            o = jnp.dot(
                p.astype(jnp.bfloat16), kv_buf[1, :, kv_lanes],
                preferred_element_type=jnp.float32,
            ) / total
            o_buf[c, :, :, lanes] = o.reshape(peers, rows, HEAD_DIM).astype(jnp.bfloat16)
            old = s_buf[...].reshape(tokens, 128)
            new = jnp.where(lane == h, top, jnp.where(lane == h + 64, total, old))
            s_buf[...] = new.reshape(peers, rows, 128)
            return carry

        lax.fori_loop(0, heads_chunk, head, 0)
        if c == chunks - 1:
            send(s_buf, stats_buf, s_send, s_recv)
            own_s.start()
        send(o_buf.at[c], got_buf.at[c], o_send.at[c], o_recv.at[c])
        copy = pltpu.make_async_copy(o_buf.at[c, me], got_buf.at[c, me], own_o_sem.at[c])
        copy.start()
        own_o.append(copy)

    own_s.wait()
    drain(stats_buf, s_recv)

    def forward(n, top):
        mine = stats_buf[n]
        top = jnp.where(fresh[n] == 1, mine, jnp.maximum(top, mine))
        top_buf[n] = top
        return top

    def backward(i, top):
        n = peers - 1 - i
        top = jnp.where(fresh[n + 1] == 1, top_buf[n], top)
        top_buf[n] = top
        return top

    def weigh(n, total):
        mine = stats_buf[n]
        w = jnp.exp(mine - top_buf[n]) * pltpu.roll(mine, 128 - 64, 1)
        w_buf[n] = w
        total = jnp.where(fresh[n] == 1, w, total + w)
        top_buf[n] = total
        return total

    def norm(i, total):
        n = peers - 1 - i
        total = jnp.where(fresh[n + 1] == 1, top_buf[n], total)
        w_buf[n] = w_buf[n] / total
        return total

    zero = jnp.zeros((rows, 128), jnp.float32)
    lax.fori_loop(0, peers, forward, zero)
    lax.fori_loop(0, peers, backward, zero)
    lax.fori_loop(0, peers, weigh, zero)
    lax.fori_loop(0, peers, norm, zero)

    outs = []
    for c in range(chunks):
        own_o[c].wait()
        drain(got_buf.at[c], o_recv.at[c])

        def visit(n, acc):
            w = w_buf[n]
            w = jnp.concatenate(
                [
                    jnp.broadcast_to(w[:, h:h + 1], (rows, HEAD_DIM))
                    for h in range(c * heads_chunk, (c + 1) * heads_chunk)
                ],
                axis=1,
            )
            mine = w * got_buf[c, n].astype(jnp.float32)
            acc = jnp.where(fresh[n] == 1, mine, acc + mine)
            run_buf[n] = acc
            return acc

        lax.fori_loop(0, peers, visit, jnp.zeros((rows, wide), jnp.float32), unroll=2)
        picked = jnp.stack([run_buf[jnp.clip(ends[doc_ids[b]] - 1, 0, peers - 1)] for b in range(blocks)], axis=0)
        out_buf[c] = jnp.swapaxes(picked, 0, 1).astype(jnp.bfloat16)
        copy = pltpu.make_async_copy(out_buf.at[c], out_hbm.at[:, :, columns(c)], out_sem.at[c])
        copy.start()
        outs.append(copy)
    drain(s_buf, s_send)
    for c in range(chunks):
        drain(send_buf.at[c], q_send.at[c])
        drain(o_buf.at[c], o_send.at[c])
        outs[c].wait()


STEPS = 16
LAG = 7
BACK = 2
GROUPS = 16
AHEAD = 8
FAR = -1e30


def merge(o1, l1, o2, l2):
    top = jnp.maximum(l1, l2)
    w1, w2 = jnp.exp(l1 - top), jnp.exp(l2 - top)
    out = (w1 * o1.astype(jnp.float32) + w2 * o2.astype(jnp.float32)) / (w1 + w2)
    return out.astype(jnp.bfloat16)


def join(l1, l2):
    top = jnp.maximum(l1, l2)
    return top + jnp.log(jnp.exp(l1 - top) + jnp.exp(l2 - top))


def to_row(col, first):
    shape = (col.shape[0], 128)
    hit = lax.broadcasted_iota(jnp.int32, shape, 1) == lax.broadcasted_iota(jnp.int32, shape, 0) + first
    return jnp.sum(jnp.where(hit, col, 0.0), axis=0, keepdims=True)


def to_col(row, first, count):
    shape = (count, 128)
    hit = lax.broadcasted_iota(jnp.int32, shape, 1) == lax.broadcasted_iota(jnp.int32, shape, 0) + first
    return jnp.sum(jnp.where(hit, row, 0.0), axis=1, keepdims=True)


def pick(parts, index):
    got = parts[0]
    for n in range(1, len(parts)):
        got = jnp.where(index == n, parts[n], got)
    return got


def line_kernel(
    counts, doc_ids, q_hbm, kv_hbm, out_hbm,
    raw, kv, blk, s1r, xs, xr, xls, xlr, cs, cr, dr, dlr, fs, fr, fls, flr,
    qt, run, lse, oh, lh, fin, turn, done, ends,
    q_ssem, q_rsem, q_own, kv_ssem, kv_rsem, kv_own, s_ssem, s_rsem, x_ssem, x_rsem, xl_ssem, xl_rsem,
    c_ssem, c_rsem, d_ssem, d_rsem, dl_ssem, dl_rsem, f_ssem, f_rsem, fl_ssem, fl_rsem,
    o_ssem, o_rsem, o_own,
):
    blocks = counts.shape[0]
    rounds = STEPS + LAG
    me = lax.axis_index("ctx")
    z, mine = me // 4, me % 4
    upper = z // 2
    hub = (z == 1) | (z == 2)
    leaf = (z == 0) | (z == 3)
    away = jnp.where((z == 0) | (z == 2), me + 4, me - 4)
    across = jnp.where(z == 1, me + 4, me - 4)
    mesh_id = pl.DeviceIdType.MESH

    def plane(k):
        return z * 4 + (mine + k) % 4, (mine + k) % 4

    barrier = pltpu.get_barrier_semaphore()
    for k in range(1, 4):
        pl.semaphore_signal(barrier, inc=1, device_id={"ctx": plane(k)[0]}, device_id_type=mesh_id)
    pl.semaphore_signal(barrier, inc=1, device_id={"ctx": away}, device_id_type=mesh_id)

    @pl.when(hub)
    def _():
        pl.semaphore_signal(barrier, inc=1, device_id={"ctx": across}, device_id_type=mesh_id)

    def lanes(i, g):
        return pl.ds(pl.multiple_of(i * 2048 + g * 128, 128), 128)

    def heads(i, h):
        return pl.ds(pl.multiple_of(i * 256 + h * 128, 128), 128)

    for g in range(GROUPS):
        pltpu.make_async_copy(q_hbm.at[:, :, lanes(mine, g)], raw.at[g, mine], q_own.at[g]).start()
    for h in range(2):
        pltpu.make_async_copy(kv_hbm.at[0, :, :, heads(mine, h)], kv.at[h, mine], kv_own.at[h]).start()

    def remote(src, dst, ssem, rsem, peer):
        pltpu.make_async_remote_copy(
            src_ref=src, dst_ref=dst, send_sem=ssem, recv_sem=rsem,
            device_id={"ctx": peer}, device_id_type=mesh_id,
        ).start()

    def wait(ref, sem):
        pltpu.make_async_copy(ref, ref, sem).wait()

    @pl.when(hub)
    def _():
        pl.semaphore_wait(barrier, 5)

    @pl.when(leaf)
    def _():
        pl.semaphore_wait(barrier, 4)

    def send_group(g):
        for k in range(1, 4):
            peer, i = plane(k)
            remote(q_hbm.at[:, :, lanes(i, g)], raw.at[g, mine], q_ssem, q_rsem.at[g], peer)

    def send_kv(h):
        for k in range(1, 4):
            peer, i = plane(k)
            remote(kv_hbm.at[0, :, :, heads(i, h)], kv.at[h, mine], kv_ssem, kv_rsem.at[h], peer)

    for g in range(AHEAD):
        send_group(g)
    send_kv(0)
    for g in range(AHEAD, GROUPS):
        send_group(g)
    send_kv(1)

    end = 0
    for j in range(blocks):
        end = end + counts[j]
        ends[j] = end

    def doc_at(n):
        doc = 0
        for j in range(blocks):
            doc = doc + (n >= ends[j]).astype(jnp.int32)
        return jnp.minimum(doc, blocks - 1)

    stop = [ends[j] for j in range(blocks)]
    start = [stop[j] - counts[j] for j in range(blocks)]
    doc_block = []
    for j in range(blocks):
        block = 0
        for b in range(1, blocks):
            block = block + jnp.where(doc_ids[b] == j, b, 0)
        doc_block.append(jnp.minimum(block, blocks - 1))

    def has(j, first):
        return (start[j] < first + 4) & (stop[j] > first)

    def last(j, first):
        return jnp.clip(stop[j] - 1 - first, 0, 3)

    def has_at(j, first):
        return (ends[j] - counts[j] < first + 4) & (ends[j] > first)

    def last_at(j, first):
        return jnp.clip(ends[j] - 1 - first, 0, 3)

    first = 4 * z
    rim = jnp.where(upper == 0, 0, 12)
    other = [jnp.where(upper == 0, (stop[j] > 8).astype(jnp.int32), (start[j] < 8).astype(jnp.int32)) == 1 for j in range(blocks)]
    page_doc = [doc_at(first + p) for p in range(4)]
    same = [None] + [page_doc[p] == page_doc[p - 1] for p in range(1, 4)]
    seam = jnp.where(upper == 0, 3, 11)
    seam_doc, mid_doc = doc_at(seam), doc_at(7)
    seam_cut = seam_doc == doc_at(seam + 1)
    mid_cut = mid_doc == doc_at(8)

    def prepare(g):
        wait(raw.at[g, mine], q_own.at[g])
        wait(raw.at[g, pl.ds(0, 3)], q_rsem.at[g])
        value = raw[g].astype(jnp.float32).reshape(32, blocks, 128)
        turn[...] = jnp.swapaxes(value, 0, 1).astype(jnp.bfloat16)
        for j in range(blocks):
            blk[g, j] = turn[doc_block[j]]

    def wait_kv(v):
        for h in range(2):
            @pl.when(v == h * (STEPS // 2))
            def _():
                wait(kv.at[h, mine], kv_own.at[h])
                wait(kv.at[h, pl.ds(0, 3)], kv_rsem.at[h])

    sub = lax.broadcasted_iota(jnp.int32, (8, 128), 0)

    def attend(v, question):
        h = v // (STEPS // 2)
        tile = jnp.zeros((8, 128), jnp.float32)
        top = total = mixed = None
        for p in range(4):
            s = lax.dot_general(
                question(p), kv[h, p, 0], (((1,), (1,)), ((), ())),
                preferred_element_type=jnp.float32,
            ) * HEAD_DIM ** (-0.5)
            t = jnp.max(s, axis=-1, keepdims=True)
            e = jnp.exp(s - t)
            n = jnp.sum(e, axis=-1, keepdims=True)
            o = jnp.dot(e.astype(jnp.bfloat16), kv[h, p, 1], preferred_element_type=jnp.float32)
            if p == 0:
                top, total, mixed = t, n, o
            else:
                before = jnp.where(same[p], top, FAR)
                top = jnp.maximum(before, t)
                a, b = jnp.exp(before - top), jnp.exp(t - top)
                total = a * total + b * n
                mixed = a * mixed + b * o
            run[v, p] = (mixed / total).astype(jnp.bfloat16)
            tile = jnp.where(sub == p, to_row(top + jnp.log(total), 0), tile)
        lse[v] = tile

    def finish(u, values):
        for j in range(blocks):
            done[j] = values[j]
        value = jnp.stack([done[doc_ids[b]].astype(jnp.float32) for b in range(blocks)], axis=0)
        fin[u] = jnp.swapaxes(value, 0, 1).astype(jnp.bfloat16)
        column = pl.ds(pl.multiple_of(mine * 2048 + u * 128, 128), 128)
        for k in range(1, 4):
            peer, i = plane(k)
            remote(fin.at[u, pl.ds(i * 8, 8)], out_hbm.at[:, :, column], o_ssem, o_rsem, peer)
        pltpu.make_async_copy(fin.at[u, pl.ds(mine * 8, 8)], out_hbm.at[:, :, column], o_own).start()

    @pl.when(leaf)
    def _():
        def pass_on(g):
            prepare(g)
            remote(blk.at[g], s1r.at[g], s_ssem, s_rsem.at[g], away)

        for g in range(AHEAD):
            pass_on(g)
        has_own = [has(j, first) for j in range(blocks)]
        last_own = [last(j, first) for j in range(blocks)]
        seam_last = last_at(seam_doc, first)

        @pl.loop(0, STEPS + LAG + 1)
        def _(t):
            @pl.when(t < STEPS)
            def _():
                wait_kv(t)
                wait(cr.at[t], c_rsem.at[t])
                attend(t, lambda p: jnp.concatenate([blk[t, page_doc[p]], cr[t, p]], axis=0))
                remote(run.at[t, :, pl.ds(32, 96)], dr.at[t], d_ssem, d_rsem.at[t], away)
                remote(lse.at[t], dlr.at[t], dl_ssem, dl_rsem.at[t], away)

            @pl.when(t < GROUPS - AHEAD)
            def _():
                pass_on(t + AHEAD)

            @pl.when(t >= LAG + 1)
            def _():
                u = t - LAG - 1
                wait(fr.at[u], f_rsem.at[u])
                wait(flr.at[u], fl_rsem.at[u])
                near = to_col(pick([lse[u, p:p + 1] for p in range(4)], seam_last), 0, 32)
                far = to_col(flr[u, 0:1], 0, 32)
                theirs = [fr[u, j] for j in range(blocks)]
                whole = merge(run[u, seam_last, 0:32], near, pick(theirs, seam_doc), far)
                values = []
                for j in range(blocks):
                    value = jnp.where(has_own[j], run[u, last_own[j], 0:32], theirs[j])
                    values.append(jnp.where(seam_cut & (seam_doc == j), whole, value))
                finish(u, values)

        wait(blk, s_ssem)
        wait(dr, d_ssem)
        wait(dlr, dl_ssem)

    @pl.when(hub)
    def _():
        last_rim = [last(b, rim) for b in range(blocks)]
        has_own = [has(b, first) for b in range(blocks)]
        last_own = [last(b, first) for b in range(blocks)]
        rim_doc = [doc_at(rim + p) for p in range(4)]
        seam_rim, seam_own = last_at(seam_doc, rim), last_at(seam_doc, first)
        mid_rim, mid_own = last_at(mid_doc, rim), last_at(mid_doc, first)
        mid_has_rim = has_at(mid_doc, rim)
        lane = lax.broadcasted_iota(jnp.int32, (1, 128), 1)

        def rows(ref, u):
            return [ref[u, p:p + 1] for p in range(4)]

        @pl.loop(0, rounds + BACK)
        def _(t):
            @pl.when((t >= LAG) & (t < rounds))
            def _():
                w = t - LAG
                wait(dr.at[w], d_rsem.at[w])
                wait(dlr.at[w], dl_rsem.at[w])
                rim_o = [dr[w, p] for p in range(4)]
                whole = merge(
                    pick(rim_o, seam_rim), to_col(pick(rows(dlr, w), seam_rim), 32, 96),
                    run[w, seam_own, 32:128], to_col(pick(rows(lse, w), seam_own), 32, 96),
                )
                for b in range(blocks):
                    value = jnp.where(has_own[b], run[w, last_own[b], 32:128], pick(rim_o, last_rim[b]))
                    oh[w, b] = jnp.where(seam_cut & (seam_doc == b), whole, value)
                near = pick(rows(lse, w), mid_own)
                far = jnp.where(mid_has_rim, pick(rows(dlr, w), mid_rim), FAR)
                lh[w] = jnp.broadcast_to(join(near, far), (8, 128))

            @pl.when(t < rounds)
            def _():
                w = jnp.maximum(t - LAG, 0)
                c = jnp.minimum(t, STEPS - 1)

                @pl.when(t < STEPS)
                def _():
                    prepare(t)

                @pl.when(t < STEPS)
                def _():
                    wait(s1r.at[t], s_rsem.at[t])

                asks = t < STEPS
                for b in range(blocks):
                    ask = other[b] & asks
                    xs[t, b, 0:32] = jnp.where(ask, s1r[c, b], oh[w, b, 32:64])
                    xs[t, b, 32:64] = jnp.where(ask, blk[c, b], oh[w, b, 64:96])
                @pl.when(t < LAG)
                def _():
                    part = pl.ds(1 - upper, blocks - 1)
                    remote(xs.at[t, part], xr.at[t, part], x_ssem, x_rsem.at[t], across)

                @pl.when((t >= LAG) & asks)
                def _():
                    xs[t, blocks] = oh[w, mid_doc, 32:96]
                    remote(xs.at[t], xr.at[t], x_ssem, x_rsem.at[t], across)

                @pl.when(t >= STEPS)
                def _():
                    part = pl.ds(upper, blocks - 1)
                    remote(xs.at[t, part], xr.at[t, part], x_ssem, x_rsem.at[t], across)

                @pl.when(t >= LAG)
                def _():
                    xls[t] = lh[w]
                    remote(xls.at[t], xlr.at[t], xl_ssem, xl_rsem.at[t], across)

            @pl.when(t >= BACK)
            def _():
                v = t - BACK
                inner = (v >= LAG) & (v < STEPS)

                @pl.when(inner)
                def _():
                    wait(xr.at[v], x_rsem.at[v])

                @pl.when(jnp.logical_not(inner))
                def _():
                    wait(xr.at[v, pl.ds(0, blocks - 1)], x_rsem.at[v])

                @pl.when(v < STEPS)
                def _():
                    for b in range(blocks):
                        qt[v, b, 0:32] = s1r[v, b]
                        qt[v, b, 32:64] = blk[v, b]
                        qt[v, b, 64:128] = xr[v, b]
                    for p in range(4):
                        cs[v, p] = qt[v, rim_doc[p], 32:128]
                    remote(cs.at[v], cr.at[v], c_ssem, c_rsem.at[v], away)

                @pl.when(v >= LAG)
                def _():
                    u = v - LAG
                    wait(xlr.at[v], xl_rsem.at[v])
                    near = jnp.where(lane < 32, pick(rows(lse, u), mid_own), lh[u, 0:1])
                    far = pltpu.roll(xlr[v, 0:1], 64, 1)
                    part = jnp.concatenate([run[u, mid_own, 0:32], oh[u, mid_doc, 0:32]], axis=0)
                    theirs = pick([xr[v, j] for j in range(blocks)], mid_doc)
                    theirs = jnp.where(v < STEPS, xr[v, blocks], theirs)
                    whole = merge(part, to_col(near, 0, 64), theirs, to_col(far, 0, 64))
                    values = []
                    for b in range(blocks):
                        cut = mid_cut & (mid_doc == b)
                        leafs = jnp.where(other[b], xr[v, b, 0:32], run[u, last_own[b], 0:32])
                        hubs = jnp.where(other[b], xr[v, b, 32:64], oh[u, b, 0:32])
                        fs[u, b] = jnp.where(cut, whole[0:32], leafs)
                        values.append(jnp.where(cut, whole[32:64], hubs))
                    tail = pick(rows(lse, u), seam_own)
                    tail = jnp.where(mid_cut & (mid_doc == seam_doc), join(tail, far), tail)
                    fls[u] = jnp.broadcast_to(tail, (8, 128))
                    remote(fs.at[u], fr.at[u], f_ssem, f_rsem.at[u], away)
                    remote(fls.at[u], flr.at[u], fl_ssem, fl_rsem.at[u], away)
                    finish(u, values)

            @pl.when((t >= LAG - 1) & (t < STEPS + LAG - 1))
            def _():
                v = t - LAG + 1
                wait_kv(v)
                attend(v, lambda p: qt[v, page_doc[p]])

        wait(xs.at[pl.ds(LAG, STEPS - LAG)], x_ssem)
        for t in range(0, rounds, STEPS):
            wait(xs.at[pl.ds(t, LAG), pl.ds(0, blocks - 1)], x_ssem)
        wait(xls.at[pl.ds(LAG, STEPS)], xl_ssem)
        wait(cs, c_ssem)
        wait(fs, f_ssem)
        wait(fls, fl_ssem)

    for g in range(GROUPS):
        wait(raw.at[g, pl.ds(0, 3)], q_ssem)
    for h in range(2):
        wait(kv.at[h, pl.ds(0, 3)], kv_ssem)
    theirs, ours = fin.at[:, pl.ds(0, 24)], fin.at[:, pl.ds(0, 8)]
    wait(theirs, o_ssem)
    wait(theirs, o_rsem)
    wait(ours, o_own)


def line_call(queries, kv_cache, page_counts, doc_ids):
    blocks = queries.shape[1]
    bf16, f32 = jnp.bfloat16, jnp.float32
    any_spec = pl.BlockSpec(memory_space=pl.ANY)
    smem_spec = pl.BlockSpec(memory_space=pltpu.SMEM)
    dma = pltpu.SemaphoreType.DMA
    rounds = STEPS + LAG
    tiles = pltpu.VMEM((STEPS, 8, 128), f32)
    mids = pltpu.VMEM((rounds, 8, 128), f32)
    pieces = pltpu.VMEM((STEPS, blocks, 32, 128), bf16)
    swaps = pltpu.VMEM((rounds, blocks + 1, 64, 128), bf16)
    quads = pltpu.VMEM((STEPS, 4, 96, 128), bf16)
    one, step, mid = dma(()), dma((STEPS,)), dma((rounds,))
    return pl.pallas_call(
        line_kernel,
        out_shape=jax.ShapeDtypeStruct(queries.shape, bf16),
        in_specs=[smem_spec, smem_spec, any_spec, any_spec],
        out_specs=any_spec,
        scratch_shapes=[
            pltpu.VMEM((GROUPS, 4, 8, blocks, 128), bf16),
            pltpu.VMEM((2, 4, 2, 512, 128), bf16),
            pieces, pieces, swaps, swaps, mids, mids,
            quads, quads, quads, tiles, pieces, pieces, tiles, tiles,
            pltpu.VMEM((STEPS, blocks, 128, 128), bf16),
            pltpu.VMEM((STEPS, 4, 128, 128), bf16),
            tiles,
            pltpu.VMEM((STEPS, blocks, 96, 128), bf16),
            tiles,
            pltpu.VMEM((STEPS, 32, blocks, 128), bf16),
            pltpu.VMEM((blocks, 32, 128), bf16),
            pltpu.VMEM((blocks, 32, 128), bf16),
            pltpu.SMEM((blocks,), jnp.int32),
            one, dma((GROUPS,)), dma((GROUPS,)), one, dma((2,)), dma((2,)),
            one, step, one, mid, one, mid,
            one, step, one, step, one, step, one, step, one, step,
            one, one, one,
        ],
        compiler_params=pltpu.CompilerParams(collective_id=1, has_side_effects=True),
    )(page_counts, doc_ids, queries, kv_cache)


def body(queries, kv_cache, page_counts, doc_ids):
    peers = lax.axis_size("ctx")
    rows, blocks, width = queries.shape
    if (peers, rows, blocks) == (16, 8, 8) and kv_cache.shape == (1, 2, 512, 1024):
        return line_call(queries, kv_cache, page_counts, doc_ids)
    assert kv_cache.shape[0] == 1 and width == 64 * HEAD_DIM
    wide = width // CHUNKS
    any_spec = pl.BlockSpec(memory_space=pl.ANY)
    smem_spec = pl.BlockSpec(memory_space=pltpu.SMEM)
    dma = pltpu.SemaphoreType.DMA
    pieces = pltpu.VMEM((CHUNKS, peers, rows, wide), jnp.bfloat16)
    stats = pltpu.VMEM((peers, rows, 128), jnp.float32)
    return pl.pallas_call(
        functools.partial(attend_kernel, peers),
        out_shape=jax.ShapeDtypeStruct(queries.shape, jnp.bfloat16),
        in_specs=[smem_spec, smem_spec, any_spec, any_spec],
        out_specs=any_spec,
        scratch_shapes=[
            pltpu.VMEM((CHUNKS, rows, blocks, wide), jnp.bfloat16),
            pltpu.VMEM((CHUNKS, blocks, rows, wide), jnp.bfloat16),
            pieces, pieces, pieces, pieces,
            stats, stats, stats, stats,
            pltpu.VMEM((peers, rows, wide), jnp.float32),
            pltpu.VMEM((CHUNKS, rows, blocks, wide), jnp.bfloat16),
            pltpu.VMEM(kv_cache.shape[1:], jnp.bfloat16),
            pltpu.SMEM((blocks,), jnp.int32),
            pltpu.SMEM((peers,), jnp.int32),
            pltpu.SMEM((peers,), jnp.int32),
            pltpu.SMEM((peers + 1,), jnp.int32),
            dma((CHUNKS,)),
            dma((CHUNKS,)), dma((CHUNKS,)), dma((CHUNKS,)), dma((CHUNKS,)),
            dma(()), dma(()), dma((CHUNKS,)), dma((CHUNKS,)), dma(()),
            dma(()), dma((CHUNKS,)),
        ],
        compiler_params=pltpu.CompilerParams(collective_id=0, has_side_effects=True),
    )(page_counts, doc_ids, queries, kv_cache)


def solution(mesh):
    placed = (
        P(("group", "ctx"), None, None),
        P(("group", "ctx"), None, None, None),
        P("group"),
        P("group"),
    )
    return jax.shard_map(
        body, mesh=mesh, in_specs=placed, out_specs=P(("group", "ctx"), None, None), check_vma=False
    )
```
